32 devices in a mesh: mom: 8 (over z, x), tm: 4 (over y, core).
Axes of the slice: x: 2, y: 2, z: 4, core: 2. Of those that a mesh axis runs over, the one named last changes fastest.
Arguments:
- source: float32 [2, 8, 1024, 512], P(None, 'mom', 'tm'), may hold values from -6 to 6
- inverse_diag: float32 [2, 8, 4, 256, 256], P(None, 'mom', 'tm'), may hold values from -0.25 to 0.25
- coupling: float32 [2, 8, 4, 256, 256], P(None, 'mom', 'tm'), may hold values from -0.21875 to 0.21875
- pair_moms: int32 [8, 8, 3], replicated, may hold values from 0 to 7, as said below
- pair_count: int32 [8], replicated, may hold values from 1 to 8
- pair_weight: int32 [8, 8], replicated, may hold values from 0 to 15
- vertex: float32 [16], replicated, may hold values from 0.02 to 0.2
Outputs:
- solved: bfloat16 [2, 8, 1024, 512], P(None, 'mom', 'tm')
- sigma: float32 [2, 8, 1024, 512], P(None, 'mom', 'tm')
The draws below stay inside these ranges and needn't reach their ends.
Inputs may be any that keep to these rules, and one draw needn't show every extreme that they name: `pair_moms`: entry (k, s) is ((k - q) mod 8, p, (p + q) mod 8) for some q and p.
All inputs are finite; a program needn't handle non-finite values.
Results may differ from the reference program's by a relative error of at most 0.0059.
Values may be sent and summed in bfloat16 or wider, within the bound.
No kernel may reach another device: no remote copies, remote signals or barrier semaphores. Data moves between devices by JAX's collectives and lax.ppermute only.
A program may use at most 64 MiB of HBM per device.

```python
import math
import jax
import jax.numpy as jnp
from jax import lax

TB = 256
COLS = 512
PAIRS = 8
NW = 16
K = 8
NB = 4
TIMES = 1024


def draw_pair_moms(key, part):
    base = jax.random.fold_in(key, 11)
    key_transfer, key_inner = jax.random.split(base)
    transfer = jax.random.randint(key_transfer, (K, PAIRS), 0, K)
    inner = jax.random.randint(key_inner, (K, PAIRS), 0, K)
    inner = inner.at[0, 0].set(0).at[1, 0].set(K - 1)
    owner = jnp.arange(K, dtype=jnp.int32)[:, None]
    return jnp.stack([(owner - transfer) % K, inner, (inner + transfer) % K], -1).astype(jnp.int32)


def draw_pair_count(key, part):
    base = jax.random.fold_in(key, 23)
    key_raw, key_hot = jax.random.split(base)
    raw = jax.random.randint(key_raw, (K,), 1, PAIRS + 1)
    hot_index = jax.random.randint(key_hot, (), 0, K)
    raw = raw.at[hot_index].set(PAIRS).at[(hot_index + 1) % K].set(1)
    return raw.astype(jnp.int32)


def with_ends(drawn, stream_key, low, top_value):
    extent = drawn.shape
    spot = [jax.random.randint(jax.random.fold_in(stream_key, axis), (), 0, extent[axis]) for axis in range(len(extent))]
    drawn = drawn.at[tuple(spot)].set(low)
    longest = extent.index(max(extent))
    spot[longest] = (spot[longest] + 1) % extent[longest]
    return drawn.at[tuple(spot)].set(top_value)


def block_levels(rng, extent, cuts, smallest, largest):
    factor_of = 1.0
    for axis_at, blocks in cuts:
        draws = jax.random.uniform(jax.random.fold_in(jax.random.fold_in(rng, 6), axis_at), (blocks,), jnp.float32, smallest / len(cuts), largest / len(cuts))
        factor_of = factor_of * jnp.repeat(jnp.exp(draws), extent[axis_at] // blocks).reshape((-1,) + (1,) * (len(extent) - 1 - axis_at))
    return factor_of


def centred(stream_key, extent, spread, bound, shards=(), held_as=jnp.bfloat16):
    array = spread * jax.random.normal(stream_key, extent, jnp.float32)
    if shards:
        array = array * block_levels(stream_key, extent, shards, -0.22, 0.18)
    return jnp.clip(array, -bound, bound).astype(held_as)


def setup_inputs(seed: int = 0) -> dict:
    splits = jax.random.split(jax.random.key(seed), 8)
    return {
        "source": centred(splits[0], (2, K, TIMES, COLS), 1.0, 6.0, ((1, 8), (2, 4)), jnp.float32),
        "inverse_diag": centred(splits[1], (2, K, NB, TB, TB), (2 * TB) ** -0.5, 0.25, ((1, 8), (2, 4)), jnp.float32),
        "coupling": centred(splits[2], (2, K, NB, TB, TB), (3 * TB) ** -0.5, 0.21875, ((1, 8), (2, 4)), jnp.float32),
        "pair_moms": draw_pair_moms(jax.random.fold_in(splits[7], 71), 0),
        "pair_count": draw_pair_count(jax.random.fold_in(splits[7], 71), 0),
        "pair_weight": with_ends(jax.random.randint(splits[5], (K, PAIRS), 0, NW), jax.random.fold_in(splits[5], 1), 0, NW - 1).astype(jnp.int32),
        "vertex": jnp.clip(jnp.exp(jax.random.uniform(splits[6], (NW,), jnp.float32, math.log(0.02), math.log(0.2))), 0.02, 0.2),
    }


def complex_mat(left, right):
    def real_mat(first, second):
        return jnp.einsum("kij,kjc->kic", first, second, precision=lax.Precision.HIGHEST)
    real_part = real_mat(left[0], right[0]) - real_mat(left[1], right[1])
    imag_part = real_mat(left[0], right[1]) + real_mat(left[1], right[0])
    return jnp.stack([real_part, imag_part])


def self_energy(greens, triples, live_count, weight_index, vertex):
    slots = triples.shape[1]
    entries = vertex.shape[0]
    table = jnp.sum(jnp.where(weight_index[..., None] == jnp.arange(entries, dtype=jnp.int32), vertex, 0.0), -1)
    live_mask = jnp.arange(slots, dtype=jnp.int32)[None, :] < live_count[:, None]
    scaled = jnp.where(live_mask, table, 0.0)
    total = jnp.zeros((2, triples.shape[0], greens.shape[2], greens.shape[3]), jnp.float32)
    for pair_slot in range(slots):
        first = jnp.take(greens, triples[:, pair_slot, 0], axis=1).astype(jnp.float32)
        second = jnp.take(greens, triples[:, pair_slot, 1], axis=1).astype(jnp.float32)
        third = jnp.take(greens, triples[:, pair_slot, 2], axis=1).astype(jnp.float32)
        prod_re = first[0] * second[0] - first[1] * second[1]
        prod_im = first[0] * second[1] + first[1] * second[0]
        term_re = prod_re * third[0] + prod_im * third[1]
        term_im = prod_im * third[0] - prod_re * third[1]
        factor = scaled[:, pair_slot][:, None, None]
        total = total + factor * jnp.stack([term_re, term_im])
    return total


def reference(source, inverse_diag, coupling, pair_moms, pair_count, pair_weight, vertex):
    driving = jnp.moveaxis(source.reshape(2, K, NB, TB, COLS), 2, 0)
    inverses = jnp.moveaxis(inverse_diag, 2, 0)
    couplings = jnp.moveaxis(coupling, 2, 0)

    def advance(previous, blocks):
        inverse, coupled, forcing = blocks
        current = complex_mat(inverse, forcing + complex_mat(coupled, previous))
        return current, current

    start_state = jnp.zeros((2, K, TB, COLS), jnp.float32)
    _, solved_blocks = lax.scan(advance, start_state, (inverses, couplings, driving))
    greens = jnp.moveaxis(solved_blocks, 0, 2).reshape(2, K, TIMES, COLS)
    solved = greens.astype(jnp.bfloat16)
    sigma = self_energy(solved, pair_moms, pair_count, pair_weight, vertex)
    return solved, sigma
```

```python
import functools

import jax
import jax.numpy as jnp
from jax import lax
from jax.experimental import pallas as pl
from jax.experimental.pallas import tpu as pltpu
from jax.sharding import PartitionSpec as P


F32 = jnp.float32
BF16 = jnp.bfloat16
CHUNKS = 2
MIB = 1 << 20


def params(mib):
    return pltpu.CompilerParams(vmem_limit_bytes=mib * MIB)


def cost(flops, moved):
    return pl.CostEstimate(flops=flops, bytes_accessed=moved, transcendentals=0)


def split(value):
    high = value.astype(BF16)
    return high, (value - high.astype(F32)).astype(BF16)


def embed(real, imag):
    return jnp.concatenate(
        [jnp.concatenate([real, -imag], 1), jnp.concatenate([imag, real], 1)], 0
    )


def dot(left, right):
    return lax.dot_general(left, right, (((1,), (0,)), ((), ())), preferred_element_type=F32)


def dot_split(left_high, left_low, right_high, right_low):
    return dot(left_high, right_high) + (dot(left_high, right_low) + dot(left_low, right_high))


def drive_kernel(inverse_ref, source_ref, *out_refs):
    high, low = split(embed(inverse_ref[0, 0, 0], inverse_ref[1, 0, 0]))
    size = inverse_ref.shape[-1]
    width = out_refs[0].shape[-1]
    for chunk, out_ref in enumerate(out_refs):
        columns = slice(chunk * width, (chunk + 1) * width)
        stacked = jnp.concatenate([source_ref[0, 0, :, columns], source_ref[1, 0, :, columns]], 0)
        result = dot_split(high, low, *split(stacked))
        out_ref[0] = result[:size]
        out_ref[1] = result[size:]


def propagator_kernel(inverse_ref, coupling_ref, high_ref, low_ref):
    size = inverse_ref.shape[-1]
    left = split(embed(inverse_ref[0, 0, 0], inverse_ref[1, 0, 0]))
    stacked = jnp.concatenate([coupling_ref[0, 0, 0], coupling_ref[1, 0, 0]], 0)
    result = dot_split(*left, *split(stacked))
    high, low = split(embed(result[:size], result[size:]))
    high_ref[...] = high
    low_ref[...] = low


def advance(high_ref, low_ref, drive_ref, incoming):
    total = incoming[0][...].astype(F32)
    for other in incoming[1:]:
        total = total + other[...].astype(F32)
    stacked = jnp.concatenate([total[0], total[1]], 0)
    return dot_split(high_ref[...], low_ref[...], *split(stacked))


def hop_kernel(high_ref, low_ref, drive_ref, *refs):
    *incoming, out_ref = refs
    size = drive_ref.shape[1]
    result = advance(high_ref, low_ref, drive_ref, incoming)
    out_ref[0] = (drive_ref[0] + result[:size]).astype(out_ref.dtype)
    out_ref[1] = (drive_ref[1] + result[size:]).astype(out_ref.dtype)


def last_kernel(count, order, me_ref, high_ref, low_ref, *refs):
    hops = (len(refs) - 2 - len(order)) // CHUNKS
    groups = [refs[chunk * hops : (chunk + 1) * hops] for chunk in range(CHUNKS)]
    solved_ref = refs[CHUNKS * hops]
    piece_refs = refs[CHUNKS * hops + 1 : -1]
    hold_ref = refs[-1]
    for chunk, (drive_ref, *incoming) in enumerate(groups):
        size, width = drive_ref.shape[1:]
        columns = slice(chunk * width, (chunk + 1) * width)
        result = advance(high_ref, low_ref, drive_ref, incoming)
        for part in range(2):
            value = drive_ref[part] + result[part * size : (part + 1) * size]
            hold_ref[part, :, columns] = value
            solved_ref[part, 0, :, columns] = value.astype(BF16)
    rows = piece_refs[0].shape[1]
    for step, piece_ref in zip(order, piece_refs):
        owner = jnp.bitwise_xor(me_ref[0], step)
        start = pl.multiple_of(owner * rows, rows)
        for part in range(2):
            piece_ref[part] = hold_ref[part, pl.ds(start, rows), :].astype(BF16)


def energy_kernel(order, targets, me_ref, triples_ref, counts_ref, weights_ref, vertex_ref, *refs):
    count = len(order)
    piece_refs = refs[:count]
    out_refs = refs[count:-1]
    hold_ref = refs[-1]
    slots = weights_ref.shape[1]
    rows, columns = piece_refs[0].shape[1:]
    for step, piece_ref in zip(order, piece_refs):
        owner = jnp.bitwise_xor(me_ref[0], step)
        hold_ref[owner] = piece_ref[...].astype(F32)
    tile = min(rows, 16)
    for step, out_ref in zip(targets, out_refs):
        mom = jnp.bitwise_xor(me_ref[0], step)
        live = jnp.minimum(counts_ref[mom], slots)
        for at in range(0, rows, tile):
            here = pl.ds(at, tile)

            def slot_step(slot, total):
                total_re, total_im = total
                first = triples_ref[mom, 3 * slot]
                second = triples_ref[mom, 3 * slot + 1]
                third = triples_ref[mom, 3 * slot + 2]
                factor = vertex_ref[weights_ref[mom, slot]]
                first_re = hold_ref[first, 0, here, :]
                first_im = hold_ref[first, 1, here, :]
                second_re = hold_ref[second, 0, here, :]
                second_im = hold_ref[second, 1, here, :]
                third_re = hold_ref[third, 0, here, :]
                third_im = hold_ref[third, 1, here, :]
                prod_re = first_re * second_re - first_im * second_im
                prod_im = first_re * second_im + first_im * second_re
                term_re = prod_re * third_re + prod_im * third_im
                term_im = prod_im * third_re - prod_re * third_im
                return total_re + factor * term_re, total_im + factor * term_im

            zero = jnp.zeros((tile, columns), F32)
            total_re, total_im = lax.fori_loop(0, live, slot_step, (zero, zero))
            out_ref[0, here, :] = total_re.astype(BF16)
            out_ref[1, here, :] = total_im.astype(BF16)


def gather_kernel(order, me_ref, *refs):
    piece_refs = refs[:-1]
    out_ref = refs[-1]
    rows = piece_refs[0].shape[1]
    for step, piece_ref in zip(order, piece_refs):
        owner = jnp.bitwise_xor(me_ref[0], step)
        start = pl.multiple_of(owner * rows, rows)
        for part in range(2):
            out_ref[part, 0, pl.ds(start, rows), :] = piece_ref[part].astype(F32)


def local(source, inverse_diag, coupling, pair_moms, pair_count, pair_weight, vertex):
    size = inverse_diag.shape[3]
    columns = source.shape[3]
    width = columns // CHUNKS
    moms = lax.axis_size("mom")
    times = lax.axis_size("tm")
    rows = size // moms
    me = lax.axis_index("mom").astype(jnp.int32).reshape(1)
    order = sorted(range(1, moms), key=lambda step: (-step.bit_length(), step))
    smem = pl.BlockSpec(memory_space=pltpu.SMEM)
    vmem = pl.BlockSpec(memory_space=pltpu.VMEM)

    drive = pl.pallas_call(
        drive_kernel,
        out_shape=[jax.ShapeDtypeStruct((2, size, width), F32)] * CHUNKS,
        in_specs=[vmem] * 2,
        out_specs=[vmem] * CHUNKS,
        compiler_params=params(24),
        cost_estimate=cost(24 * size * size * columns, 4 * 4 * size * columns),
        name="drive",
    )(inverse_diag, source)
    high, low = pl.pallas_call(
        propagator_kernel,
        out_shape=[jax.ShapeDtypeStruct((2 * size, 2 * size), BF16)] * 2,
        in_specs=[vmem] * 2,
        out_specs=[vmem] * 2,
        compiler_params=params(24),
        cost_estimate=cost(24 * size**3, 8 * 4 * size * size),
        name="propagator",
    )(inverse_diag, coupling)

    def hop(chunk, incoming, dtype):
        return pl.pallas_call(
            hop_kernel,
            out_shape=jax.ShapeDtypeStruct((2, size, width), dtype),
            in_specs=[vmem] * (3 + len(incoming)),
            out_specs=vmem,
            compiler_params=params(24),
            cost_estimate=cost(24 * size * size * width, 8 * 4 * size * width),
            name="hop",
        )(high, low, drive[chunk], *incoming)

    received = [[] for _ in range(CHUNKS)]
    for turn in range(times - 1):
        kind = F32 if turn % 2 == 0 else BF16
        for chunk in range(CHUNKS):
            if turn == 0:
                current = drive[chunk]
            else:
                current = hop(chunk, received[chunk], kind)
            received[chunk].append(lax.ppermute(current, "tm", [(turn, turn + 1)]))

    operands = []
    for chunk in range(CHUNKS):
        operands += [drive[chunk], *received[chunk]]
    everyone = [*order, 0]
    piece = jax.ShapeDtypeStruct((2, rows, columns), BF16)
    solved, *pieces = pl.pallas_call(
        functools.partial(last_kernel, moms, everyone),
        out_shape=[jax.ShapeDtypeStruct((2, 1, size, columns), BF16)] + [piece] * moms,
        in_specs=[smem] + [vmem] * (2 + len(operands)),
        out_specs=[vmem] * (1 + moms),
        scratch_shapes=[pltpu.VMEM((2, size, columns), F32)],
        compiler_params=params(24),
        cost_estimate=cost(24 * size * size * columns, 8 * 4 * size * columns),
        name="last",
    )(me, high, low, *operands)

    def swap(value, step):
        return lax.ppermute(value, "mom", [(at, at ^ step) for at in range(moms)])

    arrived = [swap(value, step) for value, step in zip(pieces, order)] + [pieces[-1]]
    triples = pair_moms.reshape(pair_moms.shape[0], -1)

    def energy(targets):
        return pl.pallas_call(
            functools.partial(energy_kernel, everyone, targets),
            out_shape=[piece] * len(targets),
            in_specs=[smem] * 5 + [vmem] * moms,
            out_specs=[vmem] * len(targets),
            scratch_shapes=[pltpu.VMEM((moms, 2, rows, columns), F32)],
            compiler_params=params(24),
            cost_estimate=cost(100 * rows * columns * 8 * len(targets), 4 * size * columns),
            name="energy",
        )(me, triples, pair_count, pair_weight, vertex, *arrived)

    groups = [everyone[at : at + max(2, moms // 4)] for at in range(0, moms, max(2, moms // 4))]
    home = []
    for targets in groups:
        for step, value in zip(targets, energy(targets)):
            home.append(swap(value, step) if step else value)
    sigma = pl.pallas_call(
        functools.partial(gather_kernel, everyone),
        out_shape=jax.ShapeDtypeStruct((2, 1, size, columns), F32),
        in_specs=[smem] + [vmem] * moms,
        out_specs=vmem,
        compiler_params=params(24),
        cost_estimate=cost(size * columns, 12 * size * columns),
        name="gather",
    )(me, *home)
    return solved, sigma


def solution(mesh):
    return jax.shard_map(
        local,
        mesh=mesh,
        in_specs=(
            P(None, "mom", "tm", None),
            P(None, "mom", "tm", None, None),
            P(None, "mom", "tm", None, None),
            P(),
            P(),
            P(),
            P(),
        ),
        out_specs=(P(None, "mom", "tm", None), P(None, "mom", "tm", None)),
        check_vma=False,
    )
```

```python
import functools

import jax
import jax.numpy as jnp
from jax import lax
from jax.experimental import pallas as pl
from jax.experimental.pallas import tpu as pltpu
from jax.sharding import PartitionSpec as P


F32 = jnp.float32
BF16 = jnp.bfloat16
CHUNKS = 2
MIB = 1 << 20


def params(mib):
    return pltpu.CompilerParams(vmem_limit_bytes=mib * MIB)


def cost(flops, moved):
    return pl.CostEstimate(flops=flops, bytes_accessed=moved, transcendentals=0)


def split(value):
    high = value.astype(BF16)
    return high, (value - high.astype(F32)).astype(BF16)


def embed(real, imag):
    return jnp.concatenate(
        [jnp.concatenate([real, -imag], 1), jnp.concatenate([imag, real], 1)], 0
    )


def dot(left, right):
    return lax.dot_general(left, right, (((1,), (0,)), ((), ())), preferred_element_type=F32)


def dot_split(left_high, left_low, right_high, right_low):
    return dot(left_high, right_high) + (dot(left_high, right_low) + dot(left_low, right_high))


def drive_kernel(inverse_ref, source_ref, *refs):
    count = len(refs) - 3
    out_refs = refs[:count]
    inverse, source, sems = refs[count:]
    size = inverse.shape[-1]
    width = out_refs[0].shape[-1]
    copies = [
        pltpu.make_async_copy(inverse_ref.at[part, 0, 0], inverse.at[part], sems.at[part])
        for part in range(2)
    ]
    for chunk in range(count):
        columns = pl.ds(chunk * width, width)
        for part in range(2):
            copies.append(
                pltpu.make_async_copy(
                    source_ref.at[part, 0, :, columns],
                    source.at[pl.ds(part * size, size), columns],
                    sems.at[len(copies)],
                )
            )
    for copy in copies:
        copy.start()
    copies[0].wait()
    copies[1].wait()
    high, low = split(embed(inverse[0], inverse[1]))
    for chunk, out_ref in enumerate(out_refs):
        copies[2 + 2 * chunk].wait()
        copies[3 + 2 * chunk].wait()
        stacked = source[:, chunk * width : (chunk + 1) * width]
        result = dot_split(high, low, *split(stacked))
        out_ref[0] = result[:size]
        out_ref[1] = result[size:]


def propagator_kernel(inverse_ref, coupling_ref, out_ref):
    size = inverse_ref.shape[-1]
    left = split(embed(inverse_ref[0, 0, 0], inverse_ref[1, 0, 0]))
    stacked = jnp.concatenate([coupling_ref[0, 0, 0], coupling_ref[1, 0, 0]], 0)
    result = dot_split(*left, *split(stacked))
    for part in range(2):
        high, low = split(result[part * size : (part + 1) * size])
        out_ref[0, part] = high
        out_ref[1, part] = low


def advance(matrix_ref, incoming_ref):
    high = embed(matrix_ref[0, 0], matrix_ref[0, 1])
    low = embed(matrix_ref[1, 0], matrix_ref[1, 1])
    stacked = jnp.concatenate([incoming_ref[0], incoming_ref[1]], 0)
    if stacked.dtype == BF16:
        return dot(high, stacked) + dot(low, stacked)
    return dot_split(high, low, *split(stacked))


def hop_kernel(matrix_ref, state_ref, incoming_ref, *out_refs):
    size = state_ref.shape[1]
    result = advance(matrix_ref, incoming_ref)
    for part in range(2):
        value = state_ref[part] + result[part * size : (part + 1) * size]
        for out_ref in out_refs:
            out_ref[part] = value.astype(out_ref.dtype)


def last_kernel(order, me_ref, matrix_ref, state_ref, incoming_ref, *refs):
    ready_refs = refs[: CHUNKS - 1]
    solved_ref = refs[CHUNKS - 1]
    piece_refs = refs[CHUNKS:-1]
    hold_ref = refs[-1]
    size, width = state_ref.shape[1:]
    result = advance(matrix_ref, incoming_ref)
    for part in range(2):
        hold_ref[part] = state_ref[part] + result[part * size : (part + 1) * size]
    rows = piece_refs[0].shape[1]
    for chunk, ref in enumerate([*ready_refs, hold_ref]):
        columns = slice(chunk * width, (chunk + 1) * width)
        for step, piece_ref in zip(order, piece_refs):
            owner = jnp.bitwise_xor(me_ref[0], step)
            start = pl.multiple_of(owner * rows, rows)
            for part in range(2):
                piece_ref[part, :, columns] = ref[part, pl.ds(start, rows), :].astype(BF16)
        for part in range(2):
            solved_ref[part, 0, :, columns] = ref[part].astype(BF16)


def energy_kernel(order, targets, me_ref, triples_ref, counts_ref, weights_ref, vertex_ref, *refs):
    count = len(order)
    piece_refs = refs[:count]
    out_refs = refs[count:-1]
    hold_ref = refs[-1]
    slots = weights_ref.shape[1]
    rows, columns = piece_refs[0].shape[1:]
    for step, piece_ref in zip(order, piece_refs):
        owner = jnp.bitwise_xor(me_ref[0], step)
        hold_ref[owner] = piece_ref[...].astype(F32)
    tile = min(rows, 16)
    for step, out_ref in zip(targets, out_refs):
        mom = jnp.bitwise_xor(me_ref[0], step)
        live = jnp.minimum(counts_ref[mom], slots)
        for at in range(0, rows, tile):
            here = pl.ds(at, tile)

            def slot_step(slot, total):
                total_re, total_im = total
                first = triples_ref[mom, 3 * slot]
                second = triples_ref[mom, 3 * slot + 1]
                third = triples_ref[mom, 3 * slot + 2]
                factor = vertex_ref[weights_ref[mom, slot]]
                first_re = hold_ref[first, 0, here, :]
                first_im = hold_ref[first, 1, here, :]
                second_re = hold_ref[second, 0, here, :]
                second_im = hold_ref[second, 1, here, :]
                third_re = hold_ref[third, 0, here, :]
                third_im = hold_ref[third, 1, here, :]
                prod_re = first_re * second_re - first_im * second_im
                prod_im = first_re * second_im + first_im * second_re
                term_re = prod_re * third_re + prod_im * third_im
                term_im = prod_im * third_re - prod_re * third_im
                return total_re + factor * term_re, total_im + factor * term_im

            zero = jnp.zeros((tile, columns), F32)
            total_re, total_im = lax.fori_loop(0, live, slot_step, (zero, zero))
            out_ref[0, here, :] = total_re.astype(BF16)
            out_ref[1, here, :] = total_im.astype(BF16)


def gather_kernel(order, me_ref, *refs):
    piece_refs = refs[:-1]
    out_ref = refs[-1]
    rows = piece_refs[0].shape[1]
    for step, piece_ref in zip(order, piece_refs):
        owner = jnp.bitwise_xor(me_ref[0], step)
        start = pl.multiple_of(owner * rows, rows)
        for part in range(2):
            out_ref[part, 0, pl.ds(start, rows), :] = piece_ref[part].astype(F32)


def step_order(moms):
    return sorted(range(1, moms), key=lambda step: (-step.bit_length(), step))


def local(source, inverse_diag, coupling, pair_moms, pair_count, pair_weight, vertex):
    size = inverse_diag.shape[3]
    columns = source.shape[3]
    width = columns // CHUNKS
    moms = lax.axis_size("mom")
    times = lax.axis_size("tm")
    rows = size // moms
    me = lax.axis_index("mom").astype(jnp.int32).reshape(1)
    order = step_order(moms)
    smem = pl.BlockSpec(memory_space=pltpu.SMEM)
    vmem = pl.BlockSpec(memory_space=pltpu.VMEM)

    drive = pl.pallas_call(
        drive_kernel,
        out_shape=[jax.ShapeDtypeStruct((2, size, width), F32)] * CHUNKS,
        in_specs=[pl.BlockSpec(memory_space=pltpu.HBM)] * 2,
        out_specs=[vmem] * CHUNKS,
        scratch_shapes=[
            pltpu.VMEM((2, size, size), F32),
            pltpu.VMEM((2 * size, columns), F32),
            pltpu.SemaphoreType.DMA((2 + 2 * CHUNKS,)),
        ],
        compiler_params=params(16),
        cost_estimate=cost(24 * size * size * columns, 4 * 4 * size * columns),
        name="drive",
    )(*(pltpu.with_memory_space_constraint(value, pltpu.HBM) for value in (inverse_diag, source)))
    matrix = pl.pallas_call(
        propagator_kernel,
        out_shape=jax.ShapeDtypeStruct((2, 2, size, size), BF16),
        in_specs=[vmem] * 2,
        out_specs=vmem,
        compiler_params=params(16),
        cost_estimate=cost(24 * size**3, 8 * 4 * size * size),
        name="propagator",
    )(inverse_diag, coupling)

    def hop(state, incoming, dtypes):
        return pl.pallas_call(
            hop_kernel,
            out_shape=[jax.ShapeDtypeStruct((2, size, width), dtype) for dtype in dtypes],
            in_specs=[vmem] * 3,
            out_specs=[vmem] * len(dtypes),
            compiler_params=params(16),
            cost_estimate=cost(24 * size * size * width, 8 * 4 * size * width),
            name="hop",
        )(matrix, state, incoming)

    state = list(drive)
    sent = list(drive)
    arrived = [None] * CHUNKS
    for turn in range(times - 1):
        for chunk in range(CHUNKS):
            if turn:
                kinds = [F32] if turn % 2 == 0 else [F32, BF16]
                outs = hop(state[chunk], arrived[chunk], kinds)
                state[chunk], sent[chunk] = outs[0], outs[-1]
            arrived[chunk] = lax.ppermute(sent[chunk], "tm", [(turn, turn + 1)])

    ready = [hop(state[chunk], arrived[chunk], [F32])[0] for chunk in range(CHUNKS - 1)]
    everyone = [*order, 0]
    piece = jax.ShapeDtypeStruct((2, rows, columns), BF16)
    solved, *pieces = pl.pallas_call(
        functools.partial(last_kernel, everyone),
        out_shape=[jax.ShapeDtypeStruct((2, 1, size, columns), BF16)] + [piece] * moms,
        in_specs=[smem] + [vmem] * (2 + CHUNKS),
        out_specs=[vmem] * (1 + moms),
        scratch_shapes=[pltpu.VMEM((2, size, width), F32)],
        compiler_params=params(16),
        cost_estimate=cost(24 * size * size * width, 8 * 4 * size * columns),
        name="last",
    )(me, matrix, state[-1], arrived[-1], *ready)

    def swap(value, step):
        return lax.ppermute(value, "mom", [(at, at ^ step) for at in range(moms)])

    arrived = [swap(value, step) for value, step in zip(pieces, order)] + [pieces[-1]]
    triples = pair_moms.reshape(pair_moms.shape[0], -1)

    def energy(targets):
        return pl.pallas_call(
            functools.partial(energy_kernel, everyone, targets),
            out_shape=[piece] * len(targets),
            in_specs=[smem] * 5 + [vmem] * moms,
            out_specs=[vmem] * len(targets),
            scratch_shapes=[pltpu.VMEM((moms, 2, rows, columns), F32)],
            compiler_params=params(16),
            cost_estimate=cost(100 * rows * columns * 8 * len(targets), 4 * size * columns),
            name="energy",
        )(me, triples, pair_count, pair_weight, vertex, *arrived)

    groups = [everyone[at : at + max(2, moms // 4)] for at in range(0, moms, max(2, moms // 4))]
    home = []
    for targets in groups:
        for step, value in zip(targets, energy(targets)):
            home.append(swap(value, step) if step else value)
    sigma = pl.pallas_call(
        functools.partial(gather_kernel, everyone),
        out_shape=jax.ShapeDtypeStruct((2, 1, size, columns), F32),
        in_specs=[smem] + [vmem] * moms,
        out_specs=vmem,
        compiler_params=params(16),
        cost_estimate=cost(size * columns, 12 * size * columns),
        name="gather",
    )(me, *home)
    return solved, sigma


def solution(mesh):
    return jax.shard_map(
        local,
        mesh=mesh,
        in_specs=(
            P(None, "mom", "tm", None),
            P(None, "mom", "tm", None, None),
            P(None, "mom", "tm", None, None),
            P(),
            P(),
            P(),
            P(),
        ),
        out_specs=(P(None, "mom", "tm", None), P(None, "mom", "tm", None)),
        check_vma=False,
    )
```

```python
import functools

import jax
import jax.numpy as jnp
from jax import lax
from jax.experimental import pallas as pl
from jax.experimental.pallas import tpu as pltpu
from jax.sharding import PartitionSpec as P


F32 = jnp.float32
BF16 = jnp.bfloat16
SHARES = (1, 1)
MIB = 1 << 20


def params(mib):
    return pltpu.CompilerParams(vmem_limit_bytes=mib * MIB)


def cost(flops, moved):
    return pl.CostEstimate(flops=flops, bytes_accessed=moved, transcendentals=0)


def split(value):
    high = value.astype(BF16)
    return high, (value - high.astype(F32)).astype(BF16)


def embed(real, imag):
    return jnp.concatenate(
        [jnp.concatenate([real, -imag], 1), jnp.concatenate([imag, real], 1)], 0
    )


def dot(left, right):
    return lax.dot_general(left, right, (((1,), (0,)), ((), ())), preferred_element_type=F32)


def dot_split(left_high, left_low, right_high, right_low):
    return dot(left_high, right_high) + (dot(left_high, right_low) + dot(left_low, right_high))


def load_kernel(inverse_ref, coupling_ref, source_ref, out_ref, inverse, coupling, *rest):
    *later, source, sems = rest
    size, _ = out_ref.shape[1:]
    moves = [(inverse_ref.at[:, 0, 0], inverse)]
    start = 0
    for target in [source, *later]:
        span = target.shape[-1]
        moves.append((source_ref.at[:, 0, :, pl.ds(start, span)], target))
        start += span
    moves.append((coupling_ref.at[:, 0, 0], coupling))
    copies = [
        pltpu.make_async_copy(origin, target, sems.at[at])
        for at, (origin, target) in enumerate(moves)
    ]
    for copy in copies:
        copy.start()
    copies[0].wait()
    high, low = split(embed(inverse[0], inverse[1]))
    copies[1].wait()
    stacked = jnp.concatenate([source[0], source[1]], 0)
    result = dot_split(high, low, *split(stacked))
    out_ref[0] = result[:size]
    out_ref[1] = result[size:]
    for copy in copies[2:]:
        copy.wait()


def drive_kernel(inverse_ref, source_ref, out_ref):
    size = inverse_ref.shape[-1]
    left = split(embed(inverse_ref[0], inverse_ref[1]))
    stacked = jnp.concatenate([source_ref[0], source_ref[1]], 0)
    result = dot_split(*left, *split(stacked))
    out_ref[0] = result[:size]
    out_ref[1] = result[size:]


def propagator_kernel(inverse_ref, coupling_ref, out_ref):
    size = inverse_ref.shape[-1]
    left = split(embed(inverse_ref[0], inverse_ref[1]))
    stacked = jnp.concatenate([coupling_ref[0], coupling_ref[1]], 0)
    result = dot_split(*left, *split(stacked))
    for part in range(2):
        high, low = split(result[part * size : (part + 1) * size])
        out_ref[0, part] = high
        out_ref[1, part] = low


def advance(matrix_ref, incoming_ref):
    high = embed(matrix_ref[0, 0], matrix_ref[0, 1])
    low = embed(matrix_ref[1, 0], matrix_ref[1, 1])
    stacked = jnp.concatenate([incoming_ref[0], incoming_ref[1]], 0)
    if stacked.dtype == BF16:
        return dot(high, stacked) + dot(low, stacked)
    return dot_split(high, low, *split(stacked))


def hop_kernel(matrix_ref, state_ref, incoming_ref, *out_refs):
    size = state_ref.shape[1]
    result = advance(matrix_ref, incoming_ref)
    for part in range(2):
        value = state_ref[part] + result[part * size : (part + 1) * size]
        for out_ref in out_refs:
            out_ref[part] = value.astype(out_ref.dtype)


def last_kernel(order, me_ref, matrix_ref, state_ref, incoming_ref, *refs):
    chunks = len(refs) - len(order)
    ready_refs = refs[: chunks - 1]
    piece_refs = refs[chunks - 1 : -1]
    hold_ref = refs[-1]
    size, _ = state_ref.shape[1:]
    result = advance(matrix_ref, incoming_ref)
    for part in range(2):
        hold_ref[part] = state_ref[part] + result[part * size : (part + 1) * size]
    rows = piece_refs[0].shape[1]
    first = 0
    for ref in [*ready_refs, hold_ref]:
        columns = slice(first, first + ref.shape[-1])
        first += ref.shape[-1]
        for step, piece_ref in zip(order, piece_refs):
            owner = jnp.bitwise_xor(me_ref[0], step)
            start = pl.multiple_of(owner * rows, rows)
            for part in range(2):
                piece_ref[part, :, columns] = ref[part, pl.ds(start, rows), :].astype(BF16)


def emit_kernel(*refs):
    *ready_refs, solved_ref = refs
    first = 0
    for ref in ready_refs:
        columns = slice(first, first + ref.shape[-1])
        first += ref.shape[-1]
        for part in range(2):
            solved_ref[part, 0, :, columns] = ref[part].astype(BF16)


def energy_kernel(order, targets, me_ref, triples_ref, counts_ref, weights_ref, vertex_ref, *refs):
    count = len(order)
    piece_refs = refs[:count]
    out_refs = refs[count:-2]
    hold_ref, sum_ref = refs[-2:]
    slots = weights_ref.shape[1]
    rows, _ = piece_refs[0].shape[1:]
    for step, piece_ref in zip(order, piece_refs):
        owner = jnp.bitwise_xor(me_ref[0], step)
        hold_ref[owner] = piece_ref[...].astype(F32)
    tile = min(rows, 8)
    for step, out_ref in zip(targets, out_refs):
        mom = jnp.bitwise_xor(me_ref[0], step)
        live = jnp.minimum(counts_ref[mom], slots)
        sum_ref[...] = jnp.zeros_like(sum_ref)

        def pair_step(pair, carry):
            entries = []
            for side in range(2):
                slot = jnp.minimum(2 * pair + side, slots - 1)
                moms = [triples_ref[mom, 3 * slot + place] for place in range(3)]
                factor = vertex_ref[weights_ref[mom, slot]]
                entries.append((moms, jnp.where(2 * pair + side < live, factor, 0.0)))
            for at in range(0, rows, tile):
                here = pl.ds(at, tile)
                total_re = sum_ref[0, here, :]
                total_im = sum_ref[1, here, :]
                for (first, second, third), factor in entries:
                    first_re = hold_ref[first, 0, here, :]
                    first_im = hold_ref[first, 1, here, :]
                    second_re = hold_ref[second, 0, here, :]
                    second_im = hold_ref[second, 1, here, :]
                    third_re = hold_ref[third, 0, here, :]
                    third_im = hold_ref[third, 1, here, :]
                    prod_re = first_re * second_re - first_im * second_im
                    prod_im = first_re * second_im + first_im * second_re
                    term_re = prod_re * third_re + prod_im * third_im
                    term_im = prod_im * third_re - prod_re * third_im
                    total_re = total_re + factor * term_re
                    total_im = total_im + factor * term_im
                sum_ref[0, here, :] = total_re
                sum_ref[1, here, :] = total_im
            return carry

        lax.fori_loop(0, (live + 1) // 2, pair_step, 0)
        out_ref[...] = sum_ref[...].astype(BF16)


def gather_kernel(order, me_ref, *refs):
    piece_refs = refs[:-1]
    out_ref = refs[-1]
    rows = piece_refs[0].shape[1]
    for step, piece_ref in zip(order, piece_refs):
        owner = jnp.bitwise_xor(me_ref[0], step)
        start = pl.multiple_of(owner * rows, rows)
        for part in range(2):
            out_ref[part, 0, pl.ds(start, rows), :] = piece_ref[part].astype(F32)


def step_order(moms):
    return sorted(range(1, moms), key=lambda step: (-step.bit_length(), step))


def local(source, inverse_diag, coupling, pair_moms, pair_count, pair_weight, vertex):
    size = inverse_diag.shape[3]
    columns = source.shape[3]
    widths = [columns * share // sum(SHARES) for share in SHARES]
    chunks = len(widths)
    moms = lax.axis_size("mom")
    times = lax.axis_size("tm")
    rows = size // moms
    me = lax.axis_index("mom").astype(jnp.int32).reshape(1)
    order = step_order(moms)
    smem = pl.BlockSpec(memory_space=pltpu.SMEM)
    vmem = pl.BlockSpec(memory_space=pltpu.VMEM)
    hbm = pl.BlockSpec(memory_space=pltpu.HBM)

    square = jax.ShapeDtypeStruct((2, size, size), F32)
    slabs = [jax.ShapeDtypeStruct((2, size, width), F32) for width in widths]
    outs = pl.pallas_call(
        load_kernel,
        out_shape=[slabs[0], square, square, *slabs[1:]],
        in_specs=[hbm] * 3,
        out_specs=[vmem] * (2 + chunks),
        scratch_shapes=[
            pltpu.VMEM((2, size, widths[0]), F32),
            pltpu.SemaphoreType.DMA((2 + chunks,)),
        ],
        compiler_params=params(16),
        cost_estimate=cost(24 * size * size * widths[0], 16 * size * columns),
        name="load",
    )(*(pltpu.with_memory_space_constraint(value, pltpu.HBM) for value in (inverse_diag, coupling, source)))
    inverse, coupled = outs[1:3]
    matrix = pl.pallas_call(
        propagator_kernel,
        out_shape=jax.ShapeDtypeStruct((2, 2, size, size), BF16),
        in_specs=[vmem] * 2,
        out_specs=vmem,
        compiler_params=params(16),
        cost_estimate=cost(24 * size**3, 8 * 4 * size * size),
        name="propagator",
    )(inverse, coupled)
    drive = [outs[0]]
    for chunk in range(1, chunks):
        drive.append(
            pl.pallas_call(
                drive_kernel,
                out_shape=slabs[chunk],
                in_specs=[vmem] * 2,
                out_specs=vmem,
                compiler_params=params(16),
                cost_estimate=cost(24 * size * size * widths[chunk], 16 * size * columns),
                name="drive",
            )(inverse, outs[2 + chunk])
        )

    def hop(state, incoming, dtypes):
        width = state.shape[-1]
        return pl.pallas_call(
            hop_kernel,
            out_shape=[jax.ShapeDtypeStruct((2, size, width), dtype) for dtype in dtypes],
            in_specs=[vmem] * 3,
            out_specs=[vmem] * len(dtypes),
            compiler_params=params(16),
            cost_estimate=cost(24 * size * size * width, 8 * 4 * size * width),
            name="hop",
        )(matrix, state, incoming)

    state = list(drive)
    sent = list(drive)
    arrived = [None] * chunks
    for turn in range(times - 1):
        for chunk in range(chunks):
            if turn:
                kinds = [F32] if turn % 2 == 0 else [F32, BF16]
                outs = hop(state[chunk], arrived[chunk], kinds)
                state[chunk], sent[chunk] = outs[0], outs[-1]
            arrived[chunk] = lax.ppermute(sent[chunk], "tm", [(turn, turn + 1)])

    ready = []
    for chunk in range(chunks - 1):
        ready.append(hop(state[chunk], arrived[chunk], [F32])[0])
    everyone = [*order, 0]
    piece = jax.ShapeDtypeStruct((2, rows, columns), BF16)
    *pieces, final = pl.pallas_call(
        functools.partial(last_kernel, everyone),
        out_shape=[piece] * moms + [slabs[-1]],
        in_specs=[smem] + [vmem] * (2 + chunks),
        out_specs=[vmem] * (1 + moms),
        compiler_params=params(16),
        cost_estimate=cost(24 * size * size * widths[-1], 8 * 4 * size * columns),
        name="last",
    )(me, matrix, state[-1], arrived[-1], *ready)
    solved = pl.pallas_call(
        emit_kernel,
        out_shape=jax.ShapeDtypeStruct((2, 1, size, columns), BF16),
        in_specs=[vmem] * chunks,
        out_specs=vmem,
        compiler_params=params(16),
        cost_estimate=cost(size * columns, 12 * size * columns),
        name="emit",
    )(*ready, final)

    def swap(value, step):
        return lax.ppermute(value, "mom", [(at, at ^ step) for at in range(moms)])

    arrived = [swap(value, step) for value, step in zip(pieces, order)] + [pieces[-1]]
    triples = pair_moms.reshape(pair_moms.shape[0], -1)

    def energy(targets):
        return pl.pallas_call(
            functools.partial(energy_kernel, everyone, targets),
            out_shape=[piece] * len(targets),
            in_specs=[smem] * 5 + [vmem] * moms,
            out_specs=[vmem] * len(targets),
            scratch_shapes=[
                pltpu.VMEM((moms, 2, rows, columns), F32),
                pltpu.VMEM((2, rows, columns), F32),
            ],
            compiler_params=params(16),
            cost_estimate=cost(100 * rows * columns * 8 * len(targets), 4 * size * columns),
            name="energy",
        )(me, triples, pair_count, pair_weight, vertex, *arrived)

    cut = moms // 4
    groups = [order[:cut], order[cut : 2 * cut], order[2 * cut :], [0]]
    home = []
    for targets in groups:
        values = energy(targets)
        for step, value in zip(targets, values):
            home.append(swap(value, step) if step else value)
    sigma = pl.pallas_call(
        functools.partial(gather_kernel, everyone),
        out_shape=jax.ShapeDtypeStruct((2, 1, size, columns), F32),
        in_specs=[smem] + [vmem] * moms,
        out_specs=vmem,
        compiler_params=params(16),
        cost_estimate=cost(size * columns, 12 * size * columns),
        name="gather",
    )(me, *home)
    return solved, sigma


def solution(mesh):
    return jax.shard_map(
        local,
        mesh=mesh,
        in_specs=(
            P(None, "mom", "tm", None),
            P(None, "mom", "tm", None, None),
            P(None, "mom", "tm", None, None),
            P(),
            P(),
            P(),
            P(),
        ),
        out_specs=(P(None, "mom", "tm", None), P(None, "mom", "tm", None)),
        check_vma=False,
    )
```

```python
import functools

import jax
import jax.numpy as jnp
from jax import lax
from jax.experimental import pallas as pl
from jax.experimental.pallas import tpu as pltpu
from jax.sharding import PartitionSpec as P


F32 = jnp.float32
BF16 = jnp.bfloat16
SHARES = (1, 1)
MIB = 1 << 20


def params(mib):
    return pltpu.CompilerParams(vmem_limit_bytes=mib * MIB)


def cost(flops, moved):
    return pl.CostEstimate(flops=flops, bytes_accessed=moved, transcendentals=0)


def split(value):
    high = value.astype(BF16)
    return high, (value - high.astype(F32)).astype(BF16)


def embed(real, imag):
    return jnp.concatenate(
        [jnp.concatenate([real, -imag], 1), jnp.concatenate([imag, real], 1)], 0
    )


def dot(left, right):
    return lax.dot_general(left, right, (((1,), (0,)), ((), ())), preferred_element_type=F32)


def dot_split(left_high, left_low, right_high, right_low):
    return dot(left_high, right_high) + (dot(left_high, right_low) + dot(left_low, right_high))


def load_kernel(inverse_ref, coupling_ref, source_ref, out_ref, inverse, coupling, *rest):
    *later, source, sems = rest
    size, _ = out_ref.shape[1:]
    moves = [(inverse_ref.at[:, 0, 0], inverse)]
    start = 0
    for target in [source, *later]:
        span = target.shape[-1]
        moves.append((source_ref.at[:, 0, :, pl.ds(start, span)], target))
        start += span
    moves.append((coupling_ref.at[:, 0, 0], coupling))
    copies = [
        pltpu.make_async_copy(origin, target, sems.at[at])
        for at, (origin, target) in enumerate(moves)
    ]
    for copy in copies:
        copy.start()
    copies[0].wait()
    high, low = split(embed(inverse[0], inverse[1]))
    copies[1].wait()
    stacked = jnp.concatenate([source[0], source[1]], 0)
    result = dot_split(high, low, *split(stacked))
    out_ref[0] = result[:size]
    out_ref[1] = result[size:]
    for copy in copies[2:]:
        copy.wait()


def drive_kernel(inverse_ref, source_ref, out_ref):
    size = inverse_ref.shape[-1]
    left = split(embed(inverse_ref[0], inverse_ref[1]))
    stacked = jnp.concatenate([source_ref[0], source_ref[1]], 0)
    result = dot_split(*left, *split(stacked))
    out_ref[0] = result[:size]
    out_ref[1] = result[size:]


def propagator_kernel(inverse_ref, coupling_ref, out_ref):
    size = inverse_ref.shape[-1]
    left = split(embed(inverse_ref[0], inverse_ref[1]))
    stacked = jnp.concatenate([coupling_ref[0], coupling_ref[1]], 0)
    result = dot_split(*left, *split(stacked))
    for part in range(2):
        high, low = split(result[part * size : (part + 1) * size])
        out_ref[0, part] = high
        out_ref[1, part] = low


def advance(matrix_ref, incoming_ref):
    high = embed(matrix_ref[0, 0], matrix_ref[0, 1])
    low = embed(matrix_ref[1, 0], matrix_ref[1, 1])
    stacked = jnp.concatenate([incoming_ref[0], incoming_ref[1]], 0)
    if stacked.dtype == BF16:
        return dot(high, stacked) + dot(low, stacked)
    return dot_split(high, low, *split(stacked))


def hop_kernel(turn, at_ref, matrix_ref, state_ref, incoming_ref, *out_refs):
    size = state_ref.shape[1]

    @pl.when(at_ref[0] == turn)
    def receive():
        result = advance(matrix_ref, incoming_ref)
        for part in range(2):
            value = state_ref[part] + result[part * size : (part + 1) * size]
            for out_ref in out_refs:
                out_ref[part] = value.astype(out_ref.dtype)

    @pl.when(at_ref[0] != turn)
    def keep():
        out_refs[0][...] = state_ref[...]


def table_kernel(*refs):
    for at in range(len(refs) // 2):
        refs[len(refs) // 2 + at][...] = refs[at][...]


def last_kernel(order, turn, me_ref, at_ref, matrix_ref, state_ref, incoming_ref, *refs):
    chunks = len(refs) - len(order)
    ready_refs = refs[: chunks - 1]
    piece_refs = refs[chunks - 1 : -1]
    hold_ref = refs[-1]
    hop_kernel(turn, at_ref, matrix_ref, state_ref, incoming_ref, hold_ref)
    rows = piece_refs[0].shape[1]
    first = 0
    for ref in [*ready_refs, hold_ref]:
        columns = slice(first, first + ref.shape[-1])
        first += ref.shape[-1]
        for step, piece_ref in zip(order, piece_refs):
            owner = jnp.bitwise_xor(me_ref[0], step)
            start = pl.multiple_of(owner * rows, rows)
            for part in range(2):
                piece_ref[part, :, columns] = ref[part, pl.ds(start, rows), :].astype(BF16)


def emit_kernel(*refs):
    *ready_refs, solved_ref = refs
    first = 0
    for ref in ready_refs:
        columns = slice(first, first + ref.shape[-1])
        first += ref.shape[-1]
        for part in range(2):
            solved_ref[part, 0, :, columns] = ref[part].astype(BF16)


def energy_kernel(order, targets, me_ref, *refs):
    count = len(order)
    piece_refs = refs[4 : 4 + count]
    out_refs = refs[4 + count : -7]
    hold_ref, sum_ref, *tables, sems = refs[-7:]
    copies = [
        pltpu.make_async_copy(origin, target, sems.at[at])
        for at, (origin, target) in enumerate(zip(refs[:4], tables))
    ]
    for copy in copies:
        copy.start()
    triples_ref, counts_ref, weights_ref, vertex_ref = tables
    slots = weights_ref.shape[1]
    rows, _ = piece_refs[0].shape[1:]
    for step, piece_ref in zip(order, piece_refs):
        owner = jnp.bitwise_xor(me_ref[0], step)
        hold_ref[owner] = piece_ref[...].astype(F32)
    for copy in copies:
        copy.wait()
    tile = min(rows, 8)
    for step, out_ref in zip(targets, out_refs):
        mom = jnp.bitwise_xor(me_ref[0], step)
        live = jnp.minimum(counts_ref[0, mom], slots)
        sum_ref[...] = jnp.zeros_like(sum_ref)

        def pair_step(pair, carry):
            entries = []
            for side in range(2):
                slot = jnp.minimum(2 * pair + side, slots - 1)
                moms = [triples_ref[mom, 3 * slot + place] for place in range(3)]
                factor = vertex_ref[0, weights_ref[mom, slot]]
                entries.append((moms, jnp.where(2 * pair + side < live, factor, 0.0)))
            for at in range(0, rows, tile):
                here = pl.ds(at, tile)
                total_re = sum_ref[0, here, :]
                total_im = sum_ref[1, here, :]
                for (first, second, third), factor in entries:
                    first_re = hold_ref[first, 0, here, :]
                    first_im = hold_ref[first, 1, here, :]
                    second_re = hold_ref[second, 0, here, :]
                    second_im = hold_ref[second, 1, here, :]
                    third_re = hold_ref[third, 0, here, :]
                    third_im = hold_ref[third, 1, here, :]
                    prod_re = first_re * second_re - first_im * second_im
                    prod_im = first_re * second_im + first_im * second_re
                    term_re = prod_re * third_re + prod_im * third_im
                    term_im = prod_im * third_re - prod_re * third_im
                    total_re = total_re + factor * term_re
                    total_im = total_im + factor * term_im
                sum_ref[0, here, :] = total_re
                sum_ref[1, here, :] = total_im
            return carry

        lax.fori_loop(0, (live + 1) // 2, pair_step, 0)
        out_ref[...] = sum_ref[...].astype(BF16)


def gather_kernel(order, me_ref, *refs):
    piece_refs = refs[:-1]
    out_ref = refs[-1]
    rows = piece_refs[0].shape[1]
    for step, piece_ref in zip(order, piece_refs):
        owner = jnp.bitwise_xor(me_ref[0], step)
        start = pl.multiple_of(owner * rows, rows)
        for part in range(2):
            out_ref[part, 0, pl.ds(start, rows), :] = piece_ref[part].astype(F32)


def step_order(moms):
    return sorted(range(1, moms), key=lambda step: (-step.bit_length(), step))


def local(source, inverse_diag, coupling, pair_moms, pair_count, pair_weight, vertex):
    size = inverse_diag.shape[3]
    columns = source.shape[3]
    widths = [columns * share // sum(SHARES) for share in SHARES]
    chunks = len(widths)
    moms = lax.axis_size("mom")
    times = lax.axis_size("tm")
    rows = size // moms
    me = lax.axis_index("mom").astype(jnp.int32).reshape(1)
    order = step_order(moms)
    smem = pl.BlockSpec(memory_space=pltpu.SMEM)
    vmem = pl.BlockSpec(memory_space=pltpu.VMEM)
    hbm = pl.BlockSpec(memory_space=pltpu.HBM)

    square = jax.ShapeDtypeStruct((2, size, size), F32)
    slabs = [jax.ShapeDtypeStruct((2, size, width), F32) for width in widths]
    outs = pl.pallas_call(
        load_kernel,
        out_shape=[slabs[0], square, square, *slabs[1:]],
        in_specs=[hbm] * 3,
        out_specs=[vmem] * (2 + chunks),
        scratch_shapes=[
            pltpu.VMEM((2, size, widths[0]), F32),
            pltpu.SemaphoreType.DMA((2 + chunks,)),
        ],
        compiler_params=params(16),
        cost_estimate=cost(24 * size * size * widths[0], 16 * size * columns),
        name="load",
    )(*(pltpu.with_memory_space_constraint(value, pltpu.HBM) for value in (inverse_diag, coupling, source)))
    inverse, coupled = outs[1:3]
    matrix = pl.pallas_call(
        propagator_kernel,
        out_shape=jax.ShapeDtypeStruct((2, 2, size, size), BF16),
        in_specs=[vmem] * 2,
        out_specs=vmem,
        compiler_params=params(16),
        cost_estimate=cost(24 * size**3, 8 * 4 * size * size),
        name="propagator",
    )(inverse, coupled)
    drive = [outs[0]]
    for chunk in range(1, chunks):
        drive.append(
            pl.pallas_call(
                drive_kernel,
                out_shape=slabs[chunk],
                in_specs=[vmem] * 2,
                out_specs=vmem,
                compiler_params=params(16),
                cost_estimate=cost(24 * size * size * widths[chunk], 16 * size * columns),
                name="drive",
            )(inverse, outs[2 + chunk])
        )

    at = lax.axis_index("tm").astype(jnp.int32).reshape(1)

    def hop(turn, state, incoming, dtypes):
        width = state.shape[-1]
        return pl.pallas_call(
            functools.partial(hop_kernel, turn),
            out_shape=[jax.ShapeDtypeStruct((2, size, width), dtype) for dtype in dtypes],
            in_specs=[smem] + [vmem] * 3,
            out_specs=[vmem] * len(dtypes),
            input_output_aliases={2: 0},
            compiler_params=params(16),
            cost_estimate=cost(24 * size * size * width, 8 * 4 * size * width),
            name="hop",
        )(at, matrix, state, incoming)

    state = list(drive)
    sent = list(drive)
    arrived = [None] * chunks
    for turn in range(times - 1):
        for chunk in range(chunks):
            if turn:
                kinds = [F32] if turn % 2 == 0 else [F32, BF16]
                outs = hop(turn, state[chunk], arrived[chunk], kinds)
                state[chunk], sent[chunk] = outs[0], outs[-1]
            arrived[chunk] = lax.ppermute(sent[chunk], "tm", [(turn, turn + 1)])

    ready = []
    for chunk in range(chunks - 1):
        ready.append(hop(times - 1, state[chunk], arrived[chunk], [F32])[0])
    everyone = [*order, 0]
    piece = jax.ShapeDtypeStruct((2, rows, columns), BF16)
    *pieces, final = pl.pallas_call(
        functools.partial(last_kernel, everyone, times - 1),
        out_shape=[piece] * moms + [slabs[-1]],
        in_specs=[smem] * 2 + [vmem] * (2 + chunks),
        out_specs=[vmem] * (1 + moms),
        input_output_aliases={3: moms},
        compiler_params=params(16),
        cost_estimate=cost(24 * size * size * widths[-1], 8 * 4 * size * columns),
        name="last",
    )(me, at, matrix, state[-1], arrived[-1], *ready)
    solved = pl.pallas_call(
        emit_kernel,
        out_shape=jax.ShapeDtypeStruct((2, 1, size, columns), BF16),
        in_specs=[vmem] * chunks,
        out_specs=vmem,
        compiler_params=params(16),
        cost_estimate=cost(size * columns, 12 * size * columns),
        name="emit",
    )(*ready, final)

    def swap(value, step):
        return lax.ppermute(value, "mom", [(at, at ^ step) for at in range(moms)])

    arrived = [swap(value, step) for value, step in zip(pieces, order)] + [pieces[-1]]
    tables = (
        pair_moms.reshape(pair_moms.shape[0], -1),
        pair_count.reshape(1, -1),
        pair_weight,
        vertex.reshape(1, -1),
    )
    tables = pl.pallas_call(
        table_kernel,
        out_shape=[jax.ShapeDtypeStruct(table.shape, table.dtype) for table in tables],
        in_specs=[vmem] * len(tables),
        out_specs=[vmem] * len(tables),
        compiler_params=params(16),
        name="tables",
    )(*tables)

    def energy(targets):
        return pl.pallas_call(
            functools.partial(energy_kernel, everyone, targets),
            out_shape=[piece] * len(targets),
            in_specs=[smem] + [vmem] * (4 + moms),
            out_specs=[vmem] * len(targets),
            scratch_shapes=[
                pltpu.VMEM((moms, 2, rows, columns), F32),
                pltpu.VMEM((2, rows, columns), F32),
                *(pltpu.SMEM(table.shape, table.dtype) for table in tables),
                pltpu.SemaphoreType.DMA((4,)),
            ],
            compiler_params=params(16),
            cost_estimate=cost(100 * rows * columns * 8 * len(targets), 4 * size * columns),
            name="energy",
        )(me, *tables, *arrived)

    cut = moms // 4
    lead = max(1, cut // 2)
    groups = [order[:lead], order[lead : 2 * cut], order[2 * cut :], [0]]
    home = []
    for targets in groups:
        values = energy(targets)
        for step, value in zip(targets, values):
            home.append(swap(value, step) if step else value)
    sigma = pl.pallas_call(
        functools.partial(gather_kernel, everyone),
        out_shape=jax.ShapeDtypeStruct((2, 1, size, columns), F32),
        in_specs=[smem] + [vmem] * moms,
        out_specs=vmem,
        compiler_params=params(16),
        cost_estimate=cost(size * columns, 12 * size * columns),
        name="gather",
    )(me, *home)
    return solved, sigma


def solution(mesh):
    return jax.shard_map(
        local,
        mesh=mesh,
        in_specs=(
            P(None, "mom", "tm", None),
            P(None, "mom", "tm", None, None),
            P(None, "mom", "tm", None, None),
            P(),
            P(),
            P(),
            P(),
        ),
        out_specs=(P(None, "mom", "tm", None), P(None, "mom", "tm", None)),
        check_vma=False,
    )
```

```python
import functools

import jax
import jax.numpy as jnp
from jax import lax
from jax.experimental import pallas as pl
from jax.experimental.pallas import tpu as pltpu
from jax.sharding import PartitionSpec as P


F32 = jnp.float32
BF16 = jnp.bfloat16
SHARES = (1, 1)
MIB = 1 << 20


def params(mib):
    return pltpu.CompilerParams(vmem_limit_bytes=mib * MIB)


def cost(flops, moved):
    return pl.CostEstimate(flops=flops, bytes_accessed=moved, transcendentals=0)


def split(value):
    high = value.astype(BF16)
    return high, (value - high.astype(F32)).astype(BF16)


def embed(real, imag):
    return jnp.concatenate(
        [jnp.concatenate([real, -imag], 1), jnp.concatenate([imag, real], 1)], 0
    )


def dot(left, right):
    return lax.dot_general(left, right, (((1,), (0,)), ((), ())), preferred_element_type=F32)


def dot_split(left_high, left_low, right_high, right_low):
    return dot(left_high, right_high) + (dot(left_high, right_low) + dot(left_low, right_high))


def load_kernel(inverse_ref, coupling_ref, source_ref, out_ref, inverse, coupling, *rest):
    *later, source, sems = rest
    size, _ = out_ref.shape[1:]
    moves = [(inverse_ref.at[:, 0, 0], inverse)]
    start = 0
    for target in [source, *later]:
        span = target.shape[-1]
        moves.append((source_ref.at[:, 0, :, pl.ds(start, span)], target))
        start += span
    moves.append((coupling_ref.at[:, 0, 0], coupling))
    copies = [
        pltpu.make_async_copy(origin, target, sems.at[at])
        for at, (origin, target) in enumerate(moves)
    ]
    for copy in copies:
        copy.start()
    copies[0].wait()
    high, low = split(embed(inverse[0], inverse[1]))
    copies[1].wait()
    stacked = jnp.concatenate([source[0], source[1]], 0)
    result = dot_split(high, low, *split(stacked))
    out_ref[0] = result[:size]
    out_ref[1] = result[size:]
    for copy in copies[2:]:
        copy.wait()


def drive_kernel(inverse_ref, source_ref, out_ref):
    size = inverse_ref.shape[-1]
    left = split(embed(inverse_ref[0], inverse_ref[1]))
    stacked = jnp.concatenate([source_ref[0], source_ref[1]], 0)
    result = dot_split(*left, *split(stacked))
    out_ref[0] = result[:size]
    out_ref[1] = result[size:]


def propagator_kernel(inverse_ref, coupling_ref, out_ref):
    size = inverse_ref.shape[-1]
    left = split(embed(inverse_ref[0], inverse_ref[1]))
    stacked = jnp.concatenate([coupling_ref[0], coupling_ref[1]], 0)
    result = dot_split(*left, *split(stacked))
    for part in range(2):
        high, low = split(result[part * size : (part + 1) * size])
        out_ref[0, part] = high
        out_ref[1, part] = low


def advance(matrix_ref, incoming_ref):
    high = embed(matrix_ref[0, 0], matrix_ref[0, 1])
    low = embed(matrix_ref[1, 0], matrix_ref[1, 1])
    stacked = jnp.concatenate([incoming_ref[0], incoming_ref[1]], 0)
    if stacked.dtype == BF16:
        return dot(high, stacked) + dot(low, stacked)
    return dot_split(high, low, *split(stacked))


def hop_kernel(turn, at_ref, matrix_ref, state_ref, incoming_ref, *out_refs):
    size = state_ref.shape[1]

    @pl.when(at_ref[0] == turn)
    def receive():
        result = advance(matrix_ref, incoming_ref)
        for part in range(2):
            value = state_ref[part] + result[part * size : (part + 1) * size]
            for out_ref in out_refs:
                out_ref[part] = value.astype(out_ref.dtype)

    @pl.when(at_ref[0] != turn)
    def keep():
        out_refs[0][...] = state_ref[...]


def table_kernel(*refs):
    for at in range(len(refs) // 2):
        refs[len(refs) // 2 + at][...] = refs[at][...]


def last_kernel(order, turn, me_ref, at_ref, matrix_ref, state_ref, incoming_ref, *refs):
    chunks = len(refs) - len(order)
    ready_refs = refs[: chunks - 1]
    piece_refs = refs[chunks - 1 : -1]
    hold_ref = refs[-1]
    hop_kernel(turn, at_ref, matrix_ref, state_ref, incoming_ref, hold_ref)
    rows = piece_refs[0].shape[1]
    first = 0
    for ref in [*ready_refs, hold_ref]:
        columns = slice(first, first + ref.shape[-1])
        first += ref.shape[-1]
        for step, piece_ref in zip(order, piece_refs):
            owner = jnp.bitwise_xor(me_ref[0], step)
            start = pl.multiple_of(owner * rows, rows)
            for part in range(2):
                piece_ref[part, :, columns] = ref[part, pl.ds(start, rows), :].astype(BF16)


def emit_kernel(*refs):
    *ready_refs, solved_ref = refs
    first = 0
    for ref in ready_refs:
        columns = slice(first, first + ref.shape[-1])
        first += ref.shape[-1]
        for part in range(2):
            solved_ref[part, 0, :, columns] = ref[part].astype(BF16)


def energy_kernel(order, targets, me_ref, *refs):
    count = len(order)
    piece_refs = refs[4 : 4 + count]
    out_refs = refs[4 + count : -7]
    hold_ref, sum_ref, *tables, sems = refs[-7:]
    copies = [
        pltpu.make_async_copy(origin, target, sems.at[at])
        for at, (origin, target) in enumerate(zip(refs[:4], tables))
    ]
    for copy in copies:
        copy.start()
    triples_ref, counts_ref, weights_ref, vertex_ref = tables
    slots = weights_ref.shape[1]
    rows, _ = piece_refs[0].shape[1:]
    for step, piece_ref in zip(order, piece_refs):
        owner = jnp.bitwise_xor(me_ref[0], step)
        hold_ref[owner] = piece_ref[...].astype(F32)
    for copy in copies:
        copy.wait()
    tile = min(rows, 8)
    for step, out_ref in zip(targets, out_refs):
        mom = jnp.bitwise_xor(me_ref[0], step)
        live = jnp.minimum(counts_ref[0, mom], slots)
        sum_ref[...] = jnp.zeros_like(sum_ref)

        def pair_step(pair, carry):
            entries = []
            for side in range(2):
                slot = jnp.minimum(2 * pair + side, slots - 1)
                moms = [triples_ref[mom, 3 * slot + place] for place in range(3)]
                factor = vertex_ref[0, weights_ref[mom, slot]]
                entries.append((moms, jnp.where(2 * pair + side < live, factor, 0.0)))
            for at in range(0, rows, tile):
                here = pl.ds(at, tile)
                total_re = sum_ref[0, here, :]
                total_im = sum_ref[1, here, :]
                for (first, second, third), factor in entries:
                    first_re = hold_ref[first, 0, here, :]
                    first_im = hold_ref[first, 1, here, :]
                    second_re = hold_ref[second, 0, here, :]
                    second_im = hold_ref[second, 1, here, :]
                    third_re = hold_ref[third, 0, here, :]
                    third_im = hold_ref[third, 1, here, :]
                    prod_re = first_re * second_re - first_im * second_im
                    prod_im = first_re * second_im + first_im * second_re
                    term_re = prod_re * third_re + prod_im * third_im
                    term_im = prod_im * third_re - prod_re * third_im
                    total_re = total_re + factor * term_re
                    total_im = total_im + factor * term_im
                sum_ref[0, here, :] = total_re
                sum_ref[1, here, :] = total_im
            return carry

        lax.fori_loop(0, (live + 1) // 2, pair_step, 0)
        out_ref[...] = sum_ref[...].astype(BF16)


def gather_kernel(order, me_ref, *refs):
    piece_refs = refs[:-1]
    out_ref = refs[-1]
    rows = piece_refs[0].shape[1]
    for step, piece_ref in zip(order, piece_refs):
        owner = jnp.bitwise_xor(me_ref[0], step)
        start = pl.multiple_of(owner * rows, rows)
        for part in range(2):
            out_ref[part, 0, pl.ds(start, rows), :] = piece_ref[part].astype(F32)


def relay_pairs(times, turn):
    if turn % 2 == 0:
        return [(block, block ^ 1) for block in range(times)]
    return [(block, (block + 1) % times) for block in range(times)]


def step_order(moms):
    return sorted(range(1, moms), key=lambda step: (-step.bit_length(), step))


def local(source, inverse_diag, coupling, pair_moms, pair_count, pair_weight, vertex):
    size = inverse_diag.shape[3]
    columns = source.shape[3]
    widths = [columns * share // sum(SHARES) for share in SHARES]
    chunks = len(widths)
    moms = lax.axis_size("mom")
    times = lax.axis_size("tm")
    rows = size // moms
    me = lax.axis_index("mom").astype(jnp.int32).reshape(1)
    order = step_order(moms)
    smem = pl.BlockSpec(memory_space=pltpu.SMEM)
    vmem = pl.BlockSpec(memory_space=pltpu.VMEM)
    hbm = pl.BlockSpec(memory_space=pltpu.HBM)

    square = jax.ShapeDtypeStruct((2, size, size), F32)
    slabs = [jax.ShapeDtypeStruct((2, size, width), F32) for width in widths]
    outs = pl.pallas_call(
        load_kernel,
        out_shape=[slabs[0], square, square, *slabs[1:]],
        in_specs=[hbm] * 3,
        out_specs=[vmem] * (2 + chunks),
        scratch_shapes=[
            pltpu.VMEM((2, size, widths[0]), F32),
            pltpu.SemaphoreType.DMA((2 + chunks,)),
        ],
        compiler_params=params(16),
        cost_estimate=cost(24 * size * size * widths[0], 16 * size * columns),
        name="load",
    )(*(pltpu.with_memory_space_constraint(value, pltpu.HBM) for value in (inverse_diag, coupling, source)))
    inverse, coupled = outs[1:3]
    matrix = pl.pallas_call(
        propagator_kernel,
        out_shape=jax.ShapeDtypeStruct((2, 2, size, size), BF16),
        in_specs=[vmem] * 2,
        out_specs=vmem,
        compiler_params=params(16),
        cost_estimate=cost(24 * size**3, 8 * 4 * size * size),
        name="propagator",
    )(inverse, coupled)
    drive = [outs[0]]
    for chunk in range(1, chunks):
        drive.append(
            pl.pallas_call(
                drive_kernel,
                out_shape=slabs[chunk],
                in_specs=[vmem] * 2,
                out_specs=vmem,
                compiler_params=params(16),
                cost_estimate=cost(24 * size * size * widths[chunk], 16 * size * columns),
                name="drive",
            )(inverse, outs[2 + chunk])
        )

    at = lax.axis_index("tm").astype(jnp.int32).reshape(1)

    def hop(turn, state, incoming, dtypes):
        width = state.shape[-1]
        return pl.pallas_call(
            functools.partial(hop_kernel, turn),
            out_shape=[jax.ShapeDtypeStruct((2, size, width), dtype) for dtype in dtypes],
            in_specs=[smem] + [vmem] * 3,
            out_specs=[vmem] * len(dtypes),
            input_output_aliases={2: 0},
            compiler_params=params(16),
            cost_estimate=cost(24 * size * size * width, 8 * 4 * size * width),
            name="hop",
        )(at, matrix, state, incoming)

    state = list(drive)
    sent = list(drive)
    arrived = [None] * chunks
    for turn in range(times - 1):
        for chunk in range(chunks):
            if turn:
                kinds = [F32] if turn % 2 == 0 else [F32, BF16]
                outs = hop(turn, state[chunk], arrived[chunk], kinds)
                state[chunk], sent[chunk] = outs[0], outs[-1]
            arrived[chunk] = lax.ppermute(sent[chunk], "tm", relay_pairs(times, turn))

    ready = []
    for chunk in range(chunks - 1):
        ready.append(hop(times - 1, state[chunk], arrived[chunk], [F32])[0])
    everyone = [*order, 0]
    piece = jax.ShapeDtypeStruct((2, rows, columns), BF16)
    *pieces, final = pl.pallas_call(
        functools.partial(last_kernel, everyone, times - 1),
        out_shape=[piece] * moms + [slabs[-1]],
        in_specs=[smem] * 2 + [vmem] * (2 + chunks),
        out_specs=[vmem] * (1 + moms),
        input_output_aliases={3: moms},
        compiler_params=params(16),
        cost_estimate=cost(24 * size * size * widths[-1], 8 * 4 * size * columns),
        name="last",
    )(me, at, matrix, state[-1], arrived[-1], *ready)
    solved = pl.pallas_call(
        emit_kernel,
        out_shape=jax.ShapeDtypeStruct((2, 1, size, columns), BF16),
        in_specs=[vmem] * chunks,
        out_specs=vmem,
        compiler_params=params(16),
        cost_estimate=cost(size * columns, 12 * size * columns),
        name="emit",
    )(*ready, final)

    def swap(value, step):
        return lax.ppermute(value, "mom", [(at, at ^ step) for at in range(moms)])

    arrived = [swap(value, step) for value, step in zip(pieces, order)] + [pieces[-1]]
    tables = (
        pair_moms.reshape(pair_moms.shape[0], -1),
        pair_count.reshape(1, -1),
        pair_weight,
        vertex.reshape(1, -1),
    )
    tables = pl.pallas_call(
        table_kernel,
        out_shape=[jax.ShapeDtypeStruct(table.shape, table.dtype) for table in tables],
        in_specs=[vmem] * len(tables),
        out_specs=[vmem] * len(tables),
        compiler_params=params(16),
        name="tables",
    )(*tables)

    def energy(targets):
        return pl.pallas_call(
            functools.partial(energy_kernel, everyone, targets),
            out_shape=[piece] * len(targets),
            in_specs=[smem] + [vmem] * (4 + moms),
            out_specs=[vmem] * len(targets),
            scratch_shapes=[
                pltpu.VMEM((moms, 2, rows, columns), F32),
                pltpu.VMEM((2, rows, columns), F32),
                *(pltpu.SMEM(table.shape, table.dtype) for table in tables),
                pltpu.SemaphoreType.DMA((4,)),
            ],
            compiler_params=params(16),
            cost_estimate=cost(100 * rows * columns * 8 * len(targets), 4 * size * columns),
            name="energy",
        )(me, *tables, *arrived)

    cut = moms // 4
    lead = max(1, cut // 2)
    groups = [order[:lead], order[lead : 2 * cut], order[2 * cut :], [0]]
    home = []
    for targets in groups:
        values = energy(targets)
        for step, value in zip(targets, values):
            home.append(swap(value, step) if step else value)
    sigma = pl.pallas_call(
        functools.partial(gather_kernel, everyone),
        out_shape=jax.ShapeDtypeStruct((2, 1, size, columns), F32),
        in_specs=[smem] + [vmem] * moms,
        out_specs=vmem,
        compiler_params=params(16),
        cost_estimate=cost(size * columns, 12 * size * columns),
        name="gather",
    )(me, *home)
    return solved, sigma


def solution(mesh):
    return jax.shard_map(
        local,
        mesh=mesh,
        in_specs=(
            P(None, "mom", "tm", None),
            P(None, "mom", "tm", None, None),
            P(None, "mom", "tm", None, None),
            P(),
            P(),
            P(),
            P(),
        ),
        out_specs=(P(None, "mom", "tm", None), P(None, "mom", "tm", None)),
        check_vma=False,
    )
```
